256 devices in a mesh: row: 8 (over y_hi, x), col: 16 (over z, core), pole: 2 (over y_lo).
Axes of the slice: x: 4, y: 4 (y_hi: 2, y_lo: 2; y = y_hi * 2 + y_lo), z: 8, core: 2. Of those that a mesh axis runs over, the one named last changes fastest.
Arguments:
- inv_block: bfloat16 [2, 16384, 16384], P('pole', 'row', 'col'), may hold values from -6 to 6
- block_masks: int32 [2, 128, 128], P(None, 'row', 'col'), may hold values 0 or 1
- panel_first: bfloat16 [2, 16384, 512], P('pole', 'row'), may hold values from -0.046875 to 0.046875
- panel_second: bfloat16 [2, 16384, 512], P('pole', 'row'), may hold values from -0.046875 to 0.046875
- diag_inverse: bfloat16 [2, 2, 512, 512], P(None, 'pole'), may hold values from -6 to 6
- weights: float32 [2], P('pole'), may hold values from 0.3 to 1.2
Outputs:
- density_panels: bfloat16 [2, 16384, 512], P(None, ('row', 'col', 'pole'))
- density_diag: float32 [2, 512, 512], replicated
The draws below stay inside these ranges and needn't reach their ends.
All inputs are finite; a program needn't handle non-finite values. No bound on the sum of `block_masks` on one device may be relied on, other than what follows from the above.
Results may differ from the reference program's by a relative error of at most 0.0043.
Values may be sent and summed in bfloat16 or wider, within the bound.
A program may use at most 64 MiB of HBM per device.

```python
import jax
import jax.numpy as jnp
from jax import lax

ORDER = 16384
WIDTH = 512
BLOCK = 128
NBLK = 128
POLES = 2


def touch_ends(array, rng, low, top_value):
    dims = array.shape
    place = [jax.random.randint(jax.random.fold_in(rng, axis), (), 0, dims[axis]) for axis in range(len(dims))]
    array = array.at[tuple(place)].set(low)
    longest = dims.index(max(dims))
    place[longest] = (place[longest] + 1) % dims[longest]
    return array.at[tuple(place)].set(top_value)


def shard_levels(stream_key, extent, split, least, top_value):
    def one(position, shards_of):
        steps = jax.random.uniform(jax.random.fold_in(jax.random.fold_in(stream_key, 6), position), (shards_of,), jnp.float32, least / len(split), top_value / len(split))
        return jnp.repeat(jnp.exp(steps), extent[position] // shards_of).reshape((-1,) + (1,) * (len(extent) - position - 1))

    level = one(*split[0])
    for cut in split[1:]:
        level = level * one(*cut)
    return level


def scatter_about(rng, shape, scale, bound, shards=(), kind=jnp.bfloat16):
    array = jax.random.normal(rng, shape, jnp.float32) * scale
    if len(shards) > 0:
        array = shard_levels(rng, shape, shards, -0.22, 0.18) * array
    return jnp.clip(array, min=-bound, max=bound).astype(kind)


def setup_inputs(seed: int = 0) -> dict:
    key_of = jax.random.split(jax.random.key(seed), 7)
    return {
        "inv_block": scatter_about(key_of[0], (POLES, ORDER, ORDER), 1.0, 6.0, ((0, 2), (1, 8), (2, 16))),
        "block_masks": touch_ends((jax.random.randint(key_of[1], (2, NBLK, NBLK), 0, 5) < 3).astype(jnp.int32), jax.random.fold_in(key_of[1], 1), 0, 1),
        "panel_first": scatter_about(key_of[2], (POLES, ORDER, WIDTH), ORDER ** -0.5, 0.046875, ((0, 2), (1, 8))),
        "panel_second": scatter_about(key_of[3], (POLES, ORDER, WIDTH), ORDER ** -0.5, 0.046875, ((0, 2), (1, 8))),
        "diag_inverse": scatter_about(key_of[4], (2, POLES, WIDTH, WIDTH), 1.0, 6.0, ((1, 2),)),
        "weights": jnp.clip(0.3 + 0.90000004 * jax.random.uniform(key_of[5], (POLES,), jnp.float32) ** shard_levels(key_of[5], (POLES,), ((0, 2),), -0.2, 0.2), 0.3, 1.2),
    }


def supernode(inv_block, mask_rows, factor, diag_inv, weights):
    dens_total = jnp.zeros((ORDER, WIDTH), jnp.float32)
    diag_total = jnp.zeros((WIDTH, WIDTH), jnp.float32)
    mask_bf = mask_rows.astype(jnp.bfloat16)[:, None, :, None]
    for pole_index in range(POLES):
        masked = (inv_block[pole_index].reshape(NBLK, BLOCK, NBLK, BLOCK) * mask_bf).reshape(ORDER, ORDER)
        product = jnp.dot(masked, factor[pole_index], preferred_element_type=jnp.float32)
        inner_term = jnp.dot(factor[pole_index].astype(jnp.float32).T, product, precision=lax.Precision.HIGHEST)
        dens_total = dens_total + weights[pole_index] * product
        diag_total = diag_total + weights[pole_index] * (diag_inv[pole_index].astype(jnp.float32) - inner_term)
    return (dens_total, diag_total)

def reference(inv_block, block_masks, panel_first, panel_second, diag_inverse, weights):
    dens_first, diag_first = supernode(inv_block, block_masks[0], panel_first, diag_inverse[0], weights)
    col_scale = jnp.sqrt(lax.optimization_barrier(jnp.mean(dens_first * dens_first, axis=0)) + 1e-06)
    rescaled = (panel_second / col_scale).astype(jnp.bfloat16)
    dens_second, diag_second = supernode(inv_block, block_masks[1], rescaled, diag_inverse[1], weights)
    return (jnp.stack([dens_first, dens_second]).astype(jnp.bfloat16), jnp.stack([diag_first, diag_second]))
```

```python
import jax
import jax.numpy as jnp
from jax import lax
from jax.experimental import pallas as pl
from jax.experimental.pallas import tpu as pltpu
from jax.sharding import PartitionSpec as P

MESH = pl.DeviceIdType.MESH
F32 = jnp.float32
BF16 = jnp.bfloat16

UNITS = 4
SUBS = 4
OFFSETS = (4, 3, 5, 2, 6, 1, 7, 0)
PLUS = (0, 1, 3, 5)
MINUS = (0, 2, 4, 6)


def rem(a, n):
    return lax.rem(a, jnp.int32(n))


def div(a, n):
    return lax.div(a, jnp.int32(n))


def kernel(
    inv_hbm, mask_ref, p0_hbm, p1_hbm, diag_hbm, w_ref,
    dens_out, diag_out,
    inv, masked, fac, relay, pan, pan_t, part, acc, xr, zs, zr, fin, ps, pr,
    dens, e_acc, es, er1, eq, er2, e3, e4, dg, dslice, dsum, dps, dpr,
    sq1, sq1r, sq2, sq3,
    load_sem, diag_sem,
    root_send, rb_recv, ax_send, ay_send, f_recv,
    x_send, x_recv, z_send, z_recv, p_send, p_recv,
    e1_send, e1_recv, e2_send, e2_recv, e3_send, e3_recv, e4_send, e4_recv, e5_send, e5_recv,
    s1_send, s1_recv, s2_send, s2_recv, s3_send, s3_recv, d_send, d_recv,
):
    row = lax.axis_index("row")
    col = lax.axis_index("col")
    p = lax.axis_index("pole")
    x, yh = rem(row, 4), div(row, 4)
    z, o = div(col, 2), rem(col, 2)
    y = yh * 2 + p
    xroot, yroot_h = rem(z, 4), div(z, 4)
    dx = rem(x - xroot + 4, 4)
    dy = rem(y - (yroot_h * 2 + 1 - p) + 8, 4)
    half = div(dy, 2)
    is_root = jnp.logical_and(dx == 0, yh == yroot_h)
    q = y * 4 + x

    def dev(x_, y_, z_, o_):
        return {"row": div(y_, 2) * 4 + x_, "col": z_ * 2 + o_, "pole": rem(y_, 2)}

    xp, xm = rem(x + 1, 4), rem(x + 3, 4)
    yp, ym = rem(y + 1, 4), rem(y + 3, 4)
    zp, zm = rem(z + 1, 8), rem(z + 7, 8)
    d_core = dev(x, y, z, 1 - o)
    d_xp, d_xm = dev(xp, y, z, o), dev(xm, y, z, o)
    d_yp, d_ym = dev(x, yp, z, o), dev(x, ym, z, o)
    d_zp, d_zm = dev(x, y, zp, o), dev(x, y, zm, o)
    d_pole = dev(x, yh * 2 + 1 - p, z, o)

    def plane(d):
        t = rem(q + d, 16)
        return dev(rem(t, 4), div(t, 4), z, o)

    def along(d):
        return dev(x, y, rem(z + d, 8), o)

    def rcopy(src, dst, ssem, rsem, to):
        return pltpu.make_async_remote_copy(
            src_ref=src, dst_ref=dst, send_sem=ssem, recv_sem=rsem, device_id=to, device_id_type=MESH
        )

    barrier = pltpu.get_barrier_semaphore()
    pl.semaphore_signal(barrier, inc=1, device_id=d_core, device_id_type=MESH)

    @pl.loop(1, 16)
    def _(d):
        pl.semaphore_signal(barrier, inc=1, device_id=plane(d), device_id_type=MESH)

    @pl.loop(1, 8)
    def _(d):
        pl.semaphore_signal(barrier, inc=1, device_id=along(d), device_id_type=MESH)

    ld_inv = pltpu.make_async_copy(inv_hbm.at[0], inv, load_sem.at[0])
    ld_p0 = pltpu.make_async_copy(p0_hbm.at[0], pan.at[0], load_sem.at[1])
    ld_p1 = pltpu.make_async_copy(p1_hbm.at[0], pan.at[1], load_sem.at[2])
    q_pole = (yh * 2 + 1 - p) * 4 + x
    ld_diag = []
    for k in range(2):
        for s, who in enumerate((q, q_pole)):
            at = pl.multiple_of(o * 256 + who * 16, 16)
            ld_diag.append(
                pltpu.make_async_copy(diag_hbm.at[k, 0, pl.ds(at, 16), :], dslice.at[k, s], diag_sem.at[k, s])
            )
    ld_inv.start()
    ld_p0.start()
    ld_p1.start()
    for c in ld_diag:
        c.start()

    w = w_ref[0]

    pl.semaphore_wait(barrier, 23)

    def root_copies(u, i):
        k, n = divmod(u, 2)
        panel = (p0_hbm, p1_hbm)[k]
        out = []
        for hf, to in ((0, d_yp), (1, d_ym)):
            at = pl.multiple_of(o * 1024 + hf * 512 + i * 128, 128)
            src = panel.at[0, pl.ds(at, 128), pl.ds(n * 256, 256)]
            out.append(rcopy(src, relay.at[u, i], root_send.at[u, i, hf], rb_recv.at[u, i], to))
        return out

    @pl.when(is_root)
    def _():
        for u in range(UNITS):
            for i in range(SUBS):
                for c in root_copies(u, i):
                    c.start()

    def y_copies(u, i):
        slot = half * SUBS + i
        return [
            rcopy(relay.at[u, i], fac.at[u, slot], ay_send.at[u, i, s], f_recv.at[u, slot], to)
            for s, to in ((0, d_yp), (1, d_ym))
        ]

    def x_copies(u, i):
        plus = rcopy(relay.at[u, i], relay.at[u, i], ax_send.at[u, i, 0], rb_recv.at[u, i], d_xp)
        minus = rcopy(relay.at[u, i], relay.at[u, i], ax_send.at[u, i, 1], rb_recv.at[u, i], d_xm)
        first = dx == 0
        if i % 2 == 0:
            return ((jnp.logical_or(first, dx == 1), plus), (first, minus))
        return ((first, plus), (jnp.logical_or(first, dx == 3), minus))

    def forward(u, i):
        rcopy(relay.at[u, i], relay.at[u, i], ax_send.at[u, i, 0], rb_recv.at[u, i], d_xp).wait_recv()
        for cond, c in x_copies(u, i):
            pl.when(cond)(c.start)
        for c in y_copies(u, i):
            c.start()

    def apply_masks(k):
        @pl.loop(0, 16)
        def _(i):
            rows = pl.ds(pl.multiple_of(i * 128, 128), 128)
            for j in range(8):
                m = jnp.full((16, 128), mask_ref[k, i, j].astype(F32), F32).astype(BF16)
                blk = inv[rows, pl.ds(j * 128, 128)].reshape(8, 16, 128)
                masked[k, rows, pl.ds(j * 128, 128)] = (blk * m[None]).reshape(128, 128)

    def transpose_panel(k):
        @pl.loop(0, 8)
        def _(i):
            at = pl.multiple_of(i * 256, 256)
            pan_t[k, :, pl.ds(at, 256)] = pan[k, pl.ds(at, 256), :].T

    def x_copy(u, j):
        zt = rem(z + OFFSETS[j], 8) if isinstance(j, int) else None
        at = pl.multiple_of(zt * 256 + (1 - o) * 128, 128)
        return rcopy(part.at[u, pl.ds(at, 128), :], xr.at[u, j], x_send.at[u, j], x_recv.at[u, j], d_core)

    def wait_factor(u):
        for slot in range(2 * SUBS):
            rcopy(relay.at[u, 0], fac.at[u, slot], ay_send.at[u, 0, 0], f_recv.at[u, slot], d_yp).wait_recv()

    def multiply(u, g):
        k = u // 2
        for j in (2 * g, 2 * g + 1):
            zt = rem(z + OFFSETS[j], 8)
            rows = pl.ds(pl.multiple_of(zt * 256, 256), 256)
            val = jnp.dot(masked[k, rows, :], fac[u].reshape(1024, 256), preferred_element_type=F32) * w
            acc[u, j] = val
            part[u, rows, :] = val.astype(BF16)
            x_copy(u, j).start()

    def inner(u):
        k, n = divmod(u, 2)

        @pl.loop(0, 2)
        def _(i):
            rows = pl.ds(pl.multiple_of(i * 256, 256), 256)
            e_acc[k, rows, pl.ds(n * 256, 256)] = jnp.dot(
                pan_t[k, rows, :], part[u], preferred_element_type=F32
            )

    def z_copy(u, d, s):
        to = (d_zp, d_zm)[d]
        rows = pl.ds(0, 64) if s == 0 else pl.ds(0, 128)
        return rcopy(
            zs.at[u, d, s, rows, :], zr.at[u, d, s, rows, :], z_send.at[u, d, s], z_recv.at[u, d, s], to
        )

    def own(u, j):
        x_copy(u, j).wait_recv()
        at = pl.multiple_of(o * 128, 128)
        return acc[u, j, pl.ds(at, 128), :] + xr[u, j].astype(F32)

    def ring(u, s):
        if s == 0:
            val = own(u, 0).astype(BF16)
            zs[u, 0, 0, 0:64, :] = val[0:64]
            zs[u, 1, 0, 0:64, :] = val[64:128]
            z_copy(u, 0, 0).start()
            z_copy(u, 1, 0).start()
            return
        for d, js in ((0, PLUS), (1, MINUS)):
            val = own(u, js[s])
            z_copy(u, d, s - 1).wait_recv()
            if s == 1:
                lo, hi = val[0:64], val[64:128]
                got = zr[u, d, 0, 0:64, :].astype(F32)
                if d == 0:
                    lo = lo + got
                else:
                    hi = hi + got
                zs[u, d, 1, 0:64, :] = lo.astype(BF16)
                zs[u, d, 1, 64:128, :] = hi.astype(BF16)
            else:
                zs[u, d, s] = (val + zr[u, d, s - 1].astype(F32)).astype(BF16)
            z_copy(u, d, s).start()

    def pole_copy(u):
        return rcopy(ps.at[u], pr.at[u], p_send.at[u], p_recv.at[u], d_pole)

    def finish(u):
        val = own(u, 7)
        z_copy(u, 0, 3).wait_recv()
        z_copy(u, 1, 3).wait_recv()
        fin[u] = val + zr[u, 0, 3].astype(F32) + zr[u, 1, 3].astype(F32)
        ps[u] = fin[u, pl.ds(pl.multiple_of((1 - p) * 64, 64), 64), :].astype(BF16)
        pole_copy(u).start()

    def pole_sum(u):
        k, n = divmod(u, 2)
        pole_copy(u).wait_recv()
        val = fin[u, pl.ds(pl.multiple_of(p * 64, 64), 64), :] + pr[u].astype(F32)
        dens[k, :, pl.ds(n * 256, 256)] = val

    def s1_copy():
        return rcopy(sq1, sq1r, s1_send.at[0], s1_recv.at[0], d_core)

    def s2_copy(d):
        return rcopy(sq2.at[z], sq2.at[z], s2_send.at[d], s2_recv.at[d], along(d))

    def s3_copy(d):
        return rcopy(sq3.at[q], sq3.at[q], s3_send.at[d], s3_recv.at[d], plane(d))

    def squares1():
        sq1[...] = jnp.zeros_like(sq1)
        for c in range(4):
            v = dens[0, :, pl.ds(c * 128, 128)]
            sq1[c : c + 1, :] = jnp.sum(v * v, axis=0, keepdims=True)
        s1_copy().start()

    def squares2():
        s1_copy().wait_recv()
        sq2[z] = sq1[...] + sq1r[...]

        @pl.loop(1, 8)
        def _(d):
            s2_copy(d).start()

    def squares3():
        @pl.loop(1, 8)
        def _(d):
            s2_copy(d).wait_recv()

        tot = sq2[0]
        for i in range(1, 8):
            tot = tot + sq2[i]
        sq3[q] = tot

        @pl.loop(1, 16)
        def _(d):
            s3_copy(d).start()

    def squares4():
        @pl.loop(1, 16)
        def _(d):
            s3_copy(d).wait_recv()

        tot = sq3[0]
        for i in range(1, 16):
            tot = tot + sq3[i]
        sq1r[...] = jnp.sqrt(tot * (1.0 / 16384.0) + 1e-6)

    def scale_row():
        return jnp.concatenate([sq1r[c : c + 1, :] for c in range(4)], axis=1)

    def d_copy(k):
        return rcopy(dps.at[k], dpr.at[k], d_send.at[k], d_recv.at[k], d_pole)

    def diag_exchange():
        for c in ld_diag:
            c.wait()
        for k in range(2):
            dsum[k] = dslice[k, 0].astype(F32) * w
            dps[k] = dslice[k, 1].astype(F32) * w
            d_copy(k).start()

    def e1_copy(k):
        return rcopy(es.at[k], er1.at[k], e1_send.at[k], e1_recv.at[k], d_core)

    def e2_copy(k, d):
        t = rem(q + d, 16)
        return rcopy(eq.at[k, t], er2.at[k, d], e2_send.at[k, d], e2_recv.at[k, d], plane(d))

    def e3_copy(k, d):
        return rcopy(e3.at[k, z], e3.at[k, z], e3_send.at[k, d], e3_recv.at[k, d], along(d))

    def e4_copy(k, d):
        return rcopy(e4.at[k], dg.at[k, o, q], e4_send.at[k, d], e4_recv.at[k, d], plane(d))

    def e5_copy(k):
        return rcopy(dg.at[k, o], dg.at[k, o], e5_send.at[k], e5_recv.at[k], d_core)

    def diag1(k):
        at = pl.multiple_of((1 - o) * 256, 256)
        es[k] = e_acc[k, pl.ds(at, 256), :].astype(BF16)
        e1_copy(k).start()

    def diag2(k):
        e1_copy(k).wait_recv()

        @pl.loop(0, 16)
        def _(t):
            at = pl.multiple_of(o * 256 + t * 16, 16)
            r = pl.ds(pl.multiple_of(t * 16, 16), 16)
            eq[k, t] = (e_acc[k, pl.ds(at, 16), :] + er1[k, r, :].astype(F32)).astype(BF16)

        @pl.loop(1, 16)
        def _(d):
            e2_copy(k, d).start()

    def diag3(k):
        @pl.loop(1, 16)
        def _(d):
            e2_copy(k, d).wait_recv()

        tot = eq[k, q].astype(F32)
        for i in range(1, 16):
            tot = tot + er2[k, i].astype(F32)
        e3[k, z] = tot.astype(BF16)

        @pl.loop(1, 8)
        def _(d):
            e3_copy(k, d).start()

    def diag4(k):
        @pl.loop(1, 8)
        def _(d):
            e3_copy(k, d).wait_recv()

        tot = e3[k, 0].astype(F32)
        for i in range(1, 8):
            tot = tot + e3[k, i].astype(F32)
        if k == 1:
            s = scale_row()
            base = o * 256 + q * 16
            ri = lax.broadcasted_iota(jnp.int32, (16, 512), 0) + base
            ci = lax.broadcasted_iota(jnp.int32, (16, 512), 1)
            s_full = jnp.broadcast_to(s, (16, 512))
            s_col = jnp.sum(jnp.where(ri == ci, s_full, 0.0), axis=1, keepdims=True)
            tot = tot / s_full / s_col
        d_copy(k).wait_recv()
        both = jnp.where(p == 0, dsum[k] + dpr[k], dpr[k] + dsum[k])
        val = (both - tot).astype(BF16)
        e4[k] = val
        dg[k, o, q] = val

        @pl.loop(1, 16)
        def _(d):
            e4_copy(k, d).start()

    def diag5(k):
        @pl.loop(1, 16)
        def _(d):
            e4_copy(k, d).wait_recv()

        e5_copy(k).start()

    def diag6(k):
        e5_copy(k).wait_recv()

    ld_inv.wait()
    apply_masks(0)
    for i in range(SUBS):
        forward(0, i)
    apply_masks(1)
    diag_exchange()
    for u in range(UNITS):
        if u < 3:
            forward(u + 1, 0)
        wait_factor(u)
        for g in range(4):
            multiply(u, g)
            if u < 3 and g < 3:
                forward(u + 1, g + 1)
        ring(u, 0)
        if u >= 1:
            ring(u - 1, 1)
        if u >= 2:
            ring(u - 2, 2)
        if u >= 3:
            ring(u - 3, 3)
        if u == 0:
            ld_p0.wait()
            transpose_panel(0)
        if u == 2:
            ld_p1.wait()
            transpose_panel(1)
        inner(u)
        if u == 1:
            diag1(0)
        if u == 2:
            diag2(0)
        if u == 3:
            diag1(1)
            diag3(0)
    ring(3, 1)
    ring(2, 2)
    ring(1, 3)
    finish(0)
    diag2(1)
    ring(3, 2)
    ring(2, 3)
    finish(1)
    pole_sum(0)
    ring(3, 3)
    pole_sum(1)
    squares1()
    diag4(0)
    finish(2)
    squares2()
    diag3(1)
    finish(3)
    pole_sum(2)
    squares3()
    diag5(0)
    pole_sum(3)
    squares4()
    diag4(1)
    dens_out[0] = dens[0].astype(BF16)
    dens_out[1] = (dens[1] / scale_row()).astype(BF16)
    diag6(0)
    diag5(1)
    diag6(1)
    diag_out[...] = dg[...]

    @pl.when(is_root)
    def _():
        for u in range(UNITS):
            for i in range(SUBS):
                for c in root_copies(u, i):
                    c.wait_send()

    for u in range(UNITS):
        for i in range(SUBS):
            for cond, c in x_copies(u, i):
                pl.when(cond)(c.wait_send)
            for c in y_copies(u, i):
                c.wait_send()
        for j in range(8):
            x_copy(u, j).wait_send()
        for d in range(2):
            for s in range(4):
                z_copy(u, d, s).wait_send()
        pole_copy(u).wait_send()
    s1_copy().wait_send()

    @pl.loop(1, 8)
    def _(d):
        s2_copy(d).wait_send()
        e3_copy(0, d).wait_send()
        e3_copy(1, d).wait_send()

    @pl.loop(1, 16)
    def _(d):
        s3_copy(d).wait_send()
        for k in range(2):
            e2_copy(k, d).wait_send()
            e4_copy(k, d).wait_send()

    for k in range(2):
        d_copy(k).wait_send()
        e1_copy(k).wait_send()
        e5_copy(k).wait_send()


def body(inv_block, block_masks, panel_first, panel_second, diag_inverse, weights):
    vmem = pltpu.VMEM
    dma = pltpu.SemaphoreType.DMA
    any_spec = pl.BlockSpec(memory_space=pl.ANY)
    smem = pl.BlockSpec(memory_space=pltpu.SMEM)
    out_vmem = pl.BlockSpec(memory_space=pltpu.VMEM)
    scratch = [
        vmem((2048, 1024), BF16),
        vmem((2, 2048, 1024), BF16),
        vmem((UNITS, 2 * SUBS, 128, 256), BF16),
        vmem((UNITS, SUBS, 128, 256), BF16),
        vmem((2, 2048, 512), BF16),
        vmem((2, 512, 2048), BF16),
        vmem((UNITS, 2048, 256), BF16),
        vmem((UNITS, 8, 256, 256), F32),
        vmem((UNITS, 8, 128, 256), BF16),
        vmem((UNITS, 2, 4, 128, 256), BF16),
        vmem((UNITS, 2, 4, 128, 256), BF16),
        vmem((UNITS, 128, 256), F32),
        vmem((UNITS, 64, 256), BF16),
        vmem((UNITS, 64, 256), BF16),
        vmem((2, 64, 512), F32),
        vmem((2, 512, 512), F32),
        vmem((2, 256, 512), BF16),
        vmem((2, 256, 512), BF16),
        vmem((2, 16, 16, 512), BF16),
        vmem((2, 16, 16, 512), BF16),
        vmem((2, 8, 16, 512), BF16),
        vmem((2, 16, 512), BF16),
        vmem((2, 2, 16, 16, 512), BF16),
        vmem((2, 2, 16, 512), BF16),
        vmem((2, 16, 512), F32),
        vmem((2, 16, 512), F32),
        vmem((2, 16, 512), F32),
        vmem((8, 128), F32),
        vmem((8, 128), F32),
        vmem((8, 8, 128), F32),
        vmem((16, 8, 128), F32),
        dma((3,)),
        dma((2, 2)),
        dma((UNITS, SUBS, 2)),
        dma((UNITS, SUBS)),
        dma((UNITS, SUBS, 2)),
        dma((UNITS, SUBS, 2)),
        dma((UNITS, 2 * SUBS)),
        dma((UNITS, 8)),
        dma((UNITS, 8)),
        dma((UNITS, 2, 4)),
        dma((UNITS, 2, 4)),
        dma((UNITS,)),
        dma((UNITS,)),
        dma((2,)),
        dma((2,)),
        dma((2, 16)),
        dma((2, 16)),
        dma((2, 8)),
        dma((2, 8)),
        dma((2, 16)),
        dma((2, 16)),
        dma((2,)),
        dma((2,)),
        dma((1,)),
        dma((1,)),
        dma((8,)),
        dma((8,)),
        dma((16,)),
        dma((16,)),
        dma((2,)),
        dma((2,)),
    ]
    dens, diag = pl.pallas_call(
        kernel,
        out_shape=(
            jax.ShapeDtypeStruct((2, 64, 512), BF16),
            jax.ShapeDtypeStruct((2, 2, 16, 16, 512), BF16),
        ),
        in_specs=[any_spec, smem, any_spec, any_spec, any_spec, smem],
        out_specs=(out_vmem, out_vmem),
        scratch_shapes=scratch,
        compiler_params=pltpu.CompilerParams(
            collective_id=0, has_side_effects=True, vmem_limit_bytes=60 * 1024 * 1024
        ),
    )(inv_block, block_masks, panel_first, panel_second, diag_inverse, weights)
    return dens, diag.reshape(2, 512, 512).astype(F32)


def solution(mesh):
    placed = (
        P("pole", "row", "col"),
        P(None, "row", "col"),
        P("pole", "row", None),
        P("pole", "row", None),
        P(None, "pole", None, None),
        P("pole"),
    )
    return jax.shard_map(
        body,
        mesh=mesh,
        in_specs=placed,
        out_specs=(P(None, ("row", "col", "pole"), None), P()),
        check_vma=False,
    )
```

```python
import jax
import jax.numpy as jnp
from jax import lax
from jax.experimental import pallas as pl
from jax.experimental.pallas import tpu as pltpu
from jax.sharding import PartitionSpec as P

MESH = pl.DeviceIdType.MESH
F32 = jnp.float32
BF16 = jnp.bfloat16

UNITS = 4
SUBS = 4
ROWS = 512 // SUBS
AHEAD = 8
LEAD_FIRST = 10
LEAD_REST = 5
OFFSETS = (4, 3, 5, 2, 6, 1, 7, 0)
PLUS = (0, 1, 3, 5)
MINUS = (0, 2, 4, 6)


def rem(a, n):
    return lax.rem(a, jnp.int32(n))


def div(a, n):
    return lax.div(a, jnp.int32(n))


def kernel(
    inv_hbm, mask_ref, p0_hbm, p1_hbm, diag_hbm, w_ref,
    dens_out, diag_out,
    inv, masked, fac, relay, pan, pan_t, part, acc, xr, zs, zr, fin, pr,
    dens, e_acc, es, er1, eq, er2, e3, e4, dg, dslice, dsum, dps, dpr,
    scale, sq2, sq3,
    here, load_sem, diag_sem,
    root_send, rb_recv, ax_send, ay_send, fill_send, f_recv,
    x_send, x_recv, z_send, z_recv, p_send, p_recv,
    e1_send, e1_recv, e2_send, e2_recv, e3_send, e3_recv, e4_send, e4_recv, e5_send, e5_recv,
    s2_send, s2_recv, s3_send, s3_recv, d_send, d_recv,
):
    row = lax.axis_index("row")
    col = lax.axis_index("col")
    p = lax.axis_index("pole")
    x, yh = rem(row, 4), div(row, 4)
    z, o = div(col, 2), rem(col, 2)
    y = yh * 2 + p
    xroot, yroot_h = rem(z, 4), div(z, 4)
    dx = rem(x - xroot + 4, 4)
    dy = rem(y - (yroot_h * 2 + 1 - p) + 8, 4)
    half = div(dy, 2)
    is_root = jnp.logical_and(dx == 0, yh == yroot_h)
    q = y * 4 + x

    def dev(x_, y_, z_, o_):
        return {"row": div(y_, 2) * 4 + x_, "col": z_ * 2 + o_, "pole": rem(y_, 2)}

    xp, xm = rem(x + 1, 4), rem(x + 3, 4)
    yp, ym = rem(y + 1, 4), rem(y + 3, 4)
    zp, zm = rem(z + 1, 8), rem(z + 7, 8)
    d_core = dev(x, y, z, 1 - o)
    d_xp, d_xm = dev(xp, y, z, o), dev(xm, y, z, o)
    d_yp, d_ym = dev(x, yp, z, o), dev(x, ym, z, o)
    d_zp, d_zm = dev(x, y, zp, o), dev(x, y, zm, o)
    d_pole = dev(x, yh * 2 + 1 - p, z, o)

    def plane(d):
        t = rem(q + d, 16)
        return dev(rem(t, 4), div(t, 4), z, o)

    def along(d):
        return dev(x, y, rem(z + d, 8), o)

    def rcopy(src, dst, ssem, rsem, to):
        return pltpu.make_async_remote_copy(
            src_ref=src, dst_ref=dst, send_sem=ssem, recv_sem=rsem, device_id=to, device_id_type=MESH
        )

    sent = []

    def send(make):
        make().start()
        sent.append(lambda: make().wait_send())

    def send_if(cond, make):
        pl.when(cond)(lambda: make().start())
        sent.append(lambda: pl.when(cond)(lambda: make().wait_send()))

    def send_all(make, n):
        pl.loop(1, n)(lambda d: make(d).start())
        sent.append(lambda: pl.loop(1, n)(lambda d: make(d).wait_send()))

    barrier = pltpu.get_barrier_semaphore()
    for to in (d_core, d_xp, d_xm, d_yp, d_ym, d_zp, d_zm):
        pl.semaphore_signal(barrier, inc=1, device_id=to, device_id_type=MESH)

    ld_inv = pltpu.make_async_copy(inv_hbm.at[0], inv, load_sem.at[0])
    ld_p0 = pltpu.make_async_copy(p0_hbm.at[0], pan.at[0], load_sem.at[1])
    ld_p1 = pltpu.make_async_copy(p1_hbm.at[0], pan.at[1], load_sem.at[2])
    q_pole = (yh * 2 + 1 - p) * 4 + x
    ld_diag = []
    for k in range(2):
        for s, who in enumerate((q, q_pole)):
            at = pl.multiple_of(o * 256 + who * 16, 16)
            ld_diag.append(
                pltpu.make_async_copy(diag_hbm.at[k, 0, pl.ds(at, 16), :], dslice.at[k, s], diag_sem.at[k, s])
            )
    ld_inv.start()
    ld_p0.start()
    ld_p1.start()
    for c in ld_diag:
        c.start()

    w = w_ref[0]

    pl.semaphore_wait(barrier, 7)

    def tell(i, *to):
        for d in to:
            pl.semaphore_signal(here.at[i], inc=1, device_id=d, device_id_type=MESH)

    def told(i):
        pl.semaphore_wait(here.at[i], 2)

    def root_copies(u, i):
        k, n = divmod(u, 2)
        panel = (p0_hbm, p1_hbm)[k]
        out = []
        for hf, to in ((0, d_yp), (1, d_ym)):
            at = pl.multiple_of(o * 1024 + hf * 512 + i * ROWS, ROWS)
            src = panel.at[0, pl.ds(at, ROWS), pl.ds(n * 256, 256)]
            out.append(rcopy(src, relay.at[u, i], root_send.at[u, i, hf], rb_recv.at[u, i], to))
        return out

    def root_start(u, i):
        for h in range(2):
            send_if(is_root, lambda h=h: root_copies(u, i)[h])

    def y_copies(u, i):
        slot = half * SUBS + i
        return [
            rcopy(relay.at[u, i], fac.at[u, slot], ay_send.at[u, i, s], f_recv.at[u, slot], to)
            for s, to in ((0, d_yp), (1, d_ym))
        ]

    def x_copy_to(u, i, h):
        to = (d_xp, d_xm)[h]
        return rcopy(relay.at[u, i], relay.at[u, i], ax_send.at[u, i, h], rb_recv.at[u, i], to)

    first = dx == 0

    def forward_first(n):
        if n >= UNITS * SUBS:
            return
        u, i = divmod(n, SUBS)
        if n + AHEAD < UNITS * SUBS:
            root_start(*divmod(n + AHEAD, SUBS))
        pl.when(first)(lambda: x_copy_to(u, i, 0).wait_recv())
        for h in range(2):
            send_if(first, lambda h=h: x_copy_to(u, i, h))

    def forward_rest(n):
        if n >= UNITS * SUBS:
            return
        u, i = divmod(n, SUBS)
        h = i % 2
        pl.when(dx != 0)(lambda: x_copy_to(u, i, 0).wait_recv())
        send_if(dx == (3 if h else 1), lambda: x_copy_to(u, i, h))
        for s in range(2):
            send_if(dx != 0, lambda s=s: y_copies(u, i)[s])

    done = [0, 0]

    def forward(t):
        t = t * SUBS // 4
        while done[0] <= t + LEAD_FIRST:
            forward_first(done[0])
            done[0] += 1
        while done[1] <= t + LEAD_REST:
            forward_rest(done[1])
            done[1] += 1

    def fill_copy(u, slot):
        to = d_xp if slot < SUBS else d_xm
        return rcopy(fac.at[u, slot], fac.at[u, slot], fill_send.at[u, slot], f_recv.at[u, slot], to)

    def root_fill(u):
        k, n = divmod(u, 2)
        panel = (p0_hbm, p1_hbm)[k]

        @pl.when(is_root)
        def _():
            for slot in range(2 * SUBS):
                at = pl.multiple_of(o * 1024 + slot * ROWS, ROWS)
                src = panel.at[0, pl.ds(at, ROWS), pl.ds(n * 256, 256)]
                pltpu.make_async_copy(src, fac.at[u, slot], f_recv.at[u, slot]).start()

    def wait_factor(u, *subs):
        for i in subs or range(SUBS):
            for slot in (i, SUBS + i):
                rcopy(relay.at[u, 0], fac.at[u, slot], ay_send.at[u, 0, 0], f_recv.at[u, slot], d_yp).wait_recv()
                side = dx == (3 if slot < SUBS else 1)
                send_if(jnp.logical_and(side, yh != yroot_h), lambda slot=slot: fill_copy(u, slot))

    def apply_masks(k):
        @pl.loop(0, 16)
        def _(i):
            rows = pl.ds(pl.multiple_of(i * 128, 128), 128)
            for j in range(8):
                m = jnp.full((16, 128), mask_ref[k, j, i].astype(F32), F32).astype(BF16)
                blk = inv[rows, pl.ds(j * 128, 128)].reshape(8, 16, 128)
                masked[k, rows, pl.ds(j * 128, 128)] = (blk * m[None]).reshape(128, 128)

    def transpose_panel(k):
        @pl.loop(0, 8)
        def _(i):
            at = pl.multiple_of(i * 256, 256)
            pan_t[k, :, pl.ds(at, 256)] = pan[k, pl.ds(at, 256), :].T

    def x_copy(u, j):
        zt = rem(z + OFFSETS[j], 8)
        at = pl.multiple_of(zt * 256 + (1 - o) * 128, 128)
        return rcopy(part.at[u, pl.ds(at, 128), :], xr.at[u, j], x_send.at[u, j], x_recv.at[u, j], d_core)

    def multiply(u):
        k = u // 2
        for j in range(8):
            zt = rem(z + OFFSETS[j], 8)
            rows = pl.ds(pl.multiple_of(zt * 256, 256), 256)
            val = jnp.dot(masked[k, rows, :], fac[u].reshape(1024, 256), preferred_element_type=F32) * w
            acc[u, j] = val
            part[u, rows, :] = val.astype(BF16)
        for j in range(8):
            send(lambda j=j: x_copy(u, j))

    def inner(u):
        k, n = divmod(u, 2)

        @pl.loop(0, 2)
        def _(i):
            rows = pl.ds(pl.multiple_of(i * 256, 256), 256)
            e_acc[k, rows, pl.ds(n * 256, 256)] = jnp.dot(
                pan_t[k, rows, :], part[u], preferred_element_type=F32
            )

    def z_copy(u, d, s):
        to = (d_zp, d_zm)[d]
        rows = pl.ds(0, 64) if s == 0 else pl.ds(0, 128)
        return rcopy(
            zs.at[u, d, s, rows, :], zr.at[u, d, s, rows, :], z_send.at[u, d, s], z_recv.at[u, d, s], to
        )

    def own(u, j):
        x_copy(u, j).wait_recv()
        at = pl.multiple_of(o * 128, 128)
        return acc[u, j, pl.ds(at, 128), :] + xr[u, j].astype(F32)

    def ring(u, s):
        if s == 0:
            val = own(u, 0).astype(BF16)
            zs[u, 0, 0, 0:64, :] = val[0:64]
            zs[u, 1, 0, 0:64, :] = val[64:128]
            send(lambda: z_copy(u, 0, 0))
            send(lambda: z_copy(u, 1, 0))
            return
        for d, js in ((0, PLUS), (1, MINUS)):
            val = own(u, js[s])
            z_copy(u, d, s - 1).wait_recv()
            if s == 1:
                lo, hi = val[0:64], val[64:128]
                got = zr[u, d, 0, 0:64, :].astype(F32)
                if d == 0:
                    lo = lo + got
                else:
                    hi = hi + got
                zs[u, d, 1, 0:64, :] = lo.astype(BF16)
                zs[u, d, 1, 64:128, :] = hi.astype(BF16)
            else:
                zs[u, d, s] = (val + zr[u, d, s - 1].astype(F32)).astype(BF16)
            send(lambda d=d: z_copy(u, d, s))

    def pole_copy(u):
        theirs = fin.at[u, pl.ds(pl.multiple_of((1 - p) * 64, 64), 64), :]
        return rcopy(theirs, pr.at[u], p_send.at[u], p_recv.at[u], d_pole)

    def finish(u):
        val = own(u, 7)
        z_copy(u, 0, 3).wait_recv()
        z_copy(u, 1, 3).wait_recv()
        fin[u] = val + zr[u, 0, 3].astype(F32) + zr[u, 1, 3].astype(F32)
        send(lambda: pole_copy(u))

    def pole_sum(u):
        k, n = divmod(u, 2)
        pole_copy(u).wait_recv()
        val = fin[u, pl.ds(pl.multiple_of(p * 64, 64), 64), :] + pr[u]
        dens[k, :, pl.ds(n * 256, 256)] = val

    def s2_copy(d):
        to = {"row": row, "col": rem(col + d, 16), "pole": p}
        return rcopy(sq2.at[col], sq2.at[col], s2_send.at[d], s2_recv.at[d], to)

    def s3_copy(d):
        return rcopy(sq3.at[q], sq3.at[q], s3_send.at[d], s3_recv.at[d], plane(d))

    def add_up(ref):
        tot = ref[0]
        for i in range(1, 16):
            tot = tot + ref[i]
        return tot

    def squares1():
        rows = []
        for c in range(4):
            v = dens[0, :, pl.ds(c * 128, 128)]
            rows.append(jnp.sum(v * v, axis=0, keepdims=True))
        rows.append(jnp.zeros((4, 128), F32))
        sq2[col] = jnp.concatenate(rows, axis=0)
        send_all(s2_copy, 16)

    def squares2():
        pl.loop(1, 16)(lambda d: s2_copy(d).wait_recv())
        sq3[q] = add_up(sq2)
        send_all(s3_copy, 16)

    def squares3():
        pl.loop(1, 16)(lambda d: s3_copy(d).wait_recv())
        scale[...] = jnp.sqrt(add_up(sq3) * (1.0 / 16384.0) + 1e-6)

    def scale_row():
        return jnp.concatenate([scale[c : c + 1, :] for c in range(4)], axis=1)

    def d_copy(k):
        return rcopy(dps.at[k], dpr.at[k], d_send.at[k], d_recv.at[k], d_pole)

    def diag_exchange():
        for c in ld_diag:
            c.wait()
        for k in range(2):
            dsum[k] = dslice[k, 0].astype(F32) * w
            dps[k] = dslice[k, 1].astype(F32) * w
            send(lambda k=k: d_copy(k))

    def e1_copy(k):
        return rcopy(es.at[k], er1.at[k], e1_send.at[k], e1_recv.at[k], d_core)

    def e2_copy(k, d):
        t = rem(q + d, 16)
        return rcopy(eq.at[k, t], er2.at[k, d], e2_send.at[k, d], e2_recv.at[k, d], plane(d))

    def e3_copy(k, d):
        return rcopy(e3.at[k, z], e3.at[k, z], e3_send.at[k, d], e3_recv.at[k, d], along(d))

    def e4_copy(k, d):
        return rcopy(e4.at[k], dg.at[k, o, q], e4_send.at[k, d], e4_recv.at[k, d], plane(d))

    def e5_copy(k):
        return rcopy(dg.at[k, o], dg.at[k, o], e5_send.at[k], e5_recv.at[k], d_core)

    def diag1(k):
        at = pl.multiple_of((1 - o) * 256, 256)
        es[k] = e_acc[k, pl.ds(at, 256), :].astype(BF16)
        send(lambda: e1_copy(k))

    def diag2(k):
        e1_copy(k).wait_recv()

        @pl.loop(0, 16)
        def _(t):
            at = pl.multiple_of(o * 256 + t * 16, 16)
            r = pl.ds(pl.multiple_of(t * 16, 16), 16)
            eq[k, t] = (e_acc[k, pl.ds(at, 16), :] + er1[k, r, :].astype(F32)).astype(BF16)

        send_all(lambda d: e2_copy(k, d), 16)

    def diag3(k):
        @pl.loop(1, 16)
        def _(d):
            e2_copy(k, d).wait_recv()

        tot = eq[k, q].astype(F32)
        for i in range(1, 16):
            tot = tot + er2[k, i].astype(F32)
        e3[k, z] = tot.astype(BF16)

        send_all(lambda d: e3_copy(k, d), 8)

    def diag4(k):
        @pl.loop(1, 8)
        def _(d):
            e3_copy(k, d).wait_recv()

        tot = e3[k, 0].astype(F32)
        for i in range(1, 8):
            tot = tot + e3[k, i].astype(F32)
        if k == 1:
            s = scale_row()
            base = o * 256 + q * 16
            ri = lax.broadcasted_iota(jnp.int32, (16, 512), 0) + base
            ci = lax.broadcasted_iota(jnp.int32, (16, 512), 1)
            s_full = jnp.broadcast_to(s, (16, 512))
            s_col = jnp.sum(jnp.where(ri == ci, s_full, 0.0), axis=1, keepdims=True)
            tot = tot / s_full / s_col
        d_copy(k).wait_recv()
        both = jnp.where(p == 0, dsum[k] + dpr[k], dpr[k] + dsum[k])
        val = (both - tot).astype(BF16)
        e4[k] = val
        dg[k, o, q] = val

        send_all(lambda d: e4_copy(k, d), 16)

    def diag5(k):
        @pl.loop(1, 16)
        def _(d):
            e4_copy(k, d).wait_recv()

        send(lambda: e5_copy(k))

    def diag6(k):
        e5_copy(k).wait_recv()

    for i in range(AHEAD):
        root_start(*divmod(i, SUBS))
    for u in range(UNITS):
        root_fill(u)
    tell(0, d_xp, d_xm)
    tell(3, d_zp, d_zm)
    ld_inv.wait()
    apply_masks(0)
    told(0)
    tell(1, d_yp, d_ym)
    told(3)
    tell(4, d_zp, d_zm)
    forward(-LEAD_REST)
    told(1)
    tell(2, d_yp, d_ym)
    told(4)
    tell(5, d_zp, d_zm)
    apply_masks(1)
    forward(1 - LEAD_REST)
    diag_exchange()
    told(2)
    told(5)
    for u in range(UNITS):
        forward(4 * u)
        wait_factor(u)
        forward(4 * u + 1)
        multiply(u)
        forward(4 * u + 2)
        if u == 3:
            inner(3)
            diag1(1)
        ring(u, 0)
        forward(4 * u + 3)
        if u >= 1:
            ring(u - 1, 1)
        if u >= 2:
            ring(u - 2, 2)
        if u >= 3:
            ring(u - 3, 3)
        if u == 0:
            ld_p0.wait()
            transpose_panel(0)
        if u == 1:
            ld_p1.wait()
            transpose_panel(1)
        if u < 3:
            inner(u)
        if u == 1:
            diag1(0)
    diag2(0)
    diag2(1)
    ring(1, 3)
    finish(0)
    ring(2, 2)
    ring(3, 1)
    finish(1)
    pole_sum(0)
    ring(2, 3)
    pole_sum(1)
    squares1()
    ring(3, 2)
    diag3(0)
    diag3(1)
    finish(2)
    ring(3, 3)
    squares2()
    pole_sum(2)
    diag4(0)
    finish(3)
    squares3()
    diag4(1)
    diag5(0)
    pole_sum(3)
    dens_out[0] = dens[0].astype(BF16)
    dens_out[1] = (dens[1] / scale_row()).astype(BF16)
    diag6(0)
    diag5(1)
    diag6(1)
    diag_out[...] = dg[...]

    for drain in sent:
        drain()


def body(inv_block, block_masks, panel_first, panel_second, diag_inverse, weights):
    vmem = pltpu.VMEM
    dma = pltpu.SemaphoreType.DMA
    any_spec = pl.BlockSpec(memory_space=pl.ANY)
    smem = pl.BlockSpec(memory_space=pltpu.SMEM)
    out_vmem = pl.BlockSpec(memory_space=pltpu.VMEM)
    scratch = [
        vmem((2048, 1024), BF16),
        vmem((2, 2048, 1024), BF16),
        vmem((UNITS, 2 * SUBS, ROWS, 256), BF16),
        vmem((UNITS, SUBS, ROWS, 256), BF16),
        vmem((2, 2048, 512), BF16),
        vmem((2, 512, 2048), BF16),
        vmem((UNITS, 2048, 256), BF16),
        vmem((UNITS, 8, 256, 256), F32),
        vmem((UNITS, 8, 128, 256), BF16),
        vmem((UNITS, 2, 4, 128, 256), BF16),
        vmem((UNITS, 2, 4, 128, 256), BF16),
        vmem((UNITS, 128, 256), F32),
        vmem((UNITS, 64, 256), F32),
        vmem((2, 64, 512), F32),
        vmem((2, 512, 512), F32),
        vmem((2, 256, 512), BF16),
        vmem((2, 256, 512), BF16),
        vmem((2, 16, 16, 512), BF16),
        vmem((2, 16, 16, 512), BF16),
        vmem((2, 8, 16, 512), BF16),
        vmem((2, 16, 512), BF16),
        vmem((2, 2, 16, 16, 512), BF16),
        vmem((2, 2, 16, 512), BF16),
        vmem((2, 16, 512), F32),
        vmem((2, 16, 512), F32),
        vmem((2, 16, 512), F32),
        vmem((8, 128), F32),
        vmem((16, 8, 128), F32),
        vmem((16, 8, 128), F32),
        pltpu.SemaphoreType.REGULAR((6,)),
        dma((3,)),
        dma((2, 2)),
        dma((UNITS, SUBS, 2)),
        dma((UNITS, SUBS)),
        dma((UNITS, SUBS, 2)),
        dma((UNITS, SUBS, 2)),
        dma((UNITS, 2 * SUBS)),
        dma((UNITS, 2 * SUBS)),
        dma((UNITS, 8)),
        dma((UNITS, 8)),
        dma((UNITS, 2, 4)),
        dma((UNITS, 2, 4)),
        dma((UNITS,)),
        dma((UNITS,)),
        dma((2,)),
        dma((2,)),
        dma((2, 16)),
        dma((2, 16)),
        dma((2, 8)),
        dma((2, 8)),
        dma((2, 16)),
        dma((2, 16)),
        dma((2,)),
        dma((2,)),
        dma((16,)),
        dma((16,)),
        dma((16,)),
        dma((16,)),
        dma((2,)),
        dma((2,)),
    ]
    dens, diag = pl.pallas_call(
        kernel,
        out_shape=(
            jax.ShapeDtypeStruct((2, 64, 512), BF16),
            jax.ShapeDtypeStruct((2, 2, 16, 16, 512), BF16),
        ),
        in_specs=[any_spec, smem, any_spec, any_spec, any_spec, smem],
        out_specs=(out_vmem, out_vmem),
        scratch_shapes=scratch,
        compiler_params=pltpu.CompilerParams(
            collective_id=0, has_side_effects=True, vmem_limit_bytes=60 * 1024 * 1024
        ),
    )(inv_block, block_masks.transpose(0, 2, 1), panel_first, panel_second, diag_inverse, weights)
    return dens, diag.reshape(2, 512, 512).astype(F32)


def solution(mesh):
    placed = (
        P("pole", "row", "col"),
        P(None, "row", "col"),
        P("pole", "row", None),
        P("pole", "row", None),
        P(None, "pole", None, None),
        P("pole"),
    )
    return jax.shard_map(
        body,
        mesh=mesh,
        in_specs=placed,
        out_specs=(P(None, ("row", "col", "pole"), None), P()),
        check_vma=False,
    )
```
